256 devices in a mesh: tm: 16 (over z, core), space: 16 (over x, y).
Axes of the slice: x: 4, y: 4, z: 8, core: 2. Of those that a mesh axis runs over, the one named last changes fastest.
Arguments:
- concentration: float32 [4, 16, 1024, 2048], P(None, 'tm', 'space'), may hold values from -5.5 to 5.5
- forcing: float32 [4, 16, 1024, 2048], P(None, 'tm', 'space'), may hold values from -5.5 to 5.5
- eigenbasis: bfloat16 [2048, 2048], replicated, may hold values from -0.125 to 0.125
- eigenvalues: float32 [2048], replicated, may hold values from -0.5 to -0.001, as said below
- settle_table: float32 [8], replicated, may hold values from 0.002 to 0.5, as said below
- fraction_class: int32 [4], replicated, may hold values from 0 to 7
- bed_mask: int32 [1024, 2048], P('space'), may hold values 0 or 1
Outputs:
- updated: float32 [4, 16, 1024, 2048], P(None, 'tm', 'space')
The draws below stay inside these ranges and needn't reach their ends.
Inputs may be any that keep to these rules, and one draw needn't show every extreme that they name: `fraction_class`: index into settle_table. `bed_mask`: 1 marks a bed cell. `eigenvalues`: negative. `settle_table`: positive.
All inputs are finite; a program needn't handle non-finite values. No bound on the sum of `bed_mask` on one device may be relied on, other than what follows from the above.
Results may differ from the reference program's by a relative error of at most 0.0055.
Values may be sent and summed in bfloat16 or wider, within the bound.
A program may use at most 64 MiB of HBM per device.

```python
import math
import jax
import jax.numpy as jnp
from jax import lax

F = 4
X = 2048
CLASSES = 8
SLICES = 16
NY = 1024


def shared_base(key):
    base = jax.random.normal(jax.random.fold_in(key, 101), (F, NY, X), jnp.float32)
    return jnp.clip(base, -5.0, 5.0)


def draw_concentration(key, part):
    base = shared_base(key)
    wiggle = jnp.clip(jax.random.normal(jax.random.fold_in(key, 202), (F, SLICES, NY, X), jnp.float32), -5.0, 5.0)
    return base[:, None] + 0.05 * wiggle


def draw_forcing(key, part):
    base = shared_base(key)
    first = (jnp.arange(SLICES) == 0).astype(jnp.float32)[None, :, None, None]
    noise = 0.1 * jnp.clip(jax.random.normal(jax.random.fold_in(key, 303), (F, SLICES, NY, X), jnp.float32), -5.0, 5.0)
    return noise + first * base[:, None]


def draw_eigenvalues(key, part):
    unit = jax.random.uniform(jax.random.fold_in(key, 404), (X,), jnp.float32)
    top = 0.5
    return -jnp.exp(math.log(0.001) + unit * (math.log(top) - math.log(0.001)))


def draw_settle_table(key, part):
    unit = jax.random.uniform(jax.random.fold_in(key, 505), (CLASSES,), jnp.float32)
    low = 0.005
    top = 0.5
    return jnp.exp(math.log(low) + unit * (math.log(top) - math.log(low)))


def with_ends(entries, stream_key, smallest, top_value):
    longest = entries.shape.index(max(entries.shape))
    spots = []
    for shift in (0, 1):
        where = [jax.random.randint(jax.random.fold_in(stream_key, axis), (), 0, length) for axis, length in enumerate(entries.shape)]
        where[longest] = (where[longest] + shift) % entries.shape[longest]
        spots.append(tuple(where))
    return entries.at[spots[0]].set(smallest).at[spots[1]].set(top_value)


def gaussian(key, dims, scale, reach, kind=jnp.bfloat16):
    return jnp.clip(scale * jax.random.normal(key, dims, jnp.float32), -reach, reach).astype(kind)


def setup_inputs(seed: int = 0) -> dict:
    arg_keys = jax.random.split(jax.random.key(seed), 8)
    concentration = draw_concentration(jax.random.fold_in(arg_keys[7], 71), 0)
    forcing = draw_forcing(jax.random.fold_in(arg_keys[7], 71), 0)
    eigenbasis = gaussian(arg_keys[2], (X, X), X ** -0.5, 0.125)
    eigenvalues = draw_eigenvalues(jax.random.fold_in(arg_keys[7], 71), 0)
    settle_table = draw_settle_table(jax.random.fold_in(arg_keys[7], 71), 0)
    fraction_class = with_ends(jax.random.randint(arg_keys[5], (F,), 0, CLASSES), jax.random.fold_in(arg_keys[5], 1), 0, CLASSES - 1).astype(jnp.int32)
    bed_mask = with_ends((jax.random.randint(arg_keys[6], (NY, X), 0, 4) < 1).astype(jnp.int32), jax.random.fold_in(arg_keys[6], 1), 0, 1)
    return dict(concentration=concentration, forcing=forcing, eigenbasis=eigenbasis, eigenvalues=eigenvalues, settle_table=settle_table, fraction_class=fraction_class, bed_mask=bed_mask)


CIRCULANT_ALPHA = 0.5
VERTICAL_DIFFUSION = 0.06
DEPOSITION = 0.1


def twiddles(first_index, second_index, length):
    products = (first_index[:, None] * second_index[None, :]) % length
    angle_grid = (2.0 * math.pi / length) * products.astype(jnp.float32)
    return jnp.cos(angle_grid), jnp.sin(angle_grid)


def apply_table(table, values):
    return jnp.einsum("kn,fnrx->fkrx", table, values.astype(jnp.float32), precision=lax.Precision.HIGHEST)


def to_space(modal, eigenbasis):
    return lax.dot_general(modal, eigenbasis, (((1,), (1,)), ((), ())), preferred_element_type=jnp.float32)


def solve_shifted(real_part, imag_part, freq_index, length, decay_ratio, eigenbasis, eigenvalues, diagonal):
    layout = real_part.shape
    columns = layout[-1]
    stacked = jnp.concatenate([real_part, imag_part], axis=0).astype(jnp.bfloat16).reshape(-1, columns)
    modal = jnp.dot(stacked, eigenbasis, preferred_element_type=jnp.float32).reshape((2,) + layout)
    angles = (2.0 * math.pi / length) * freq_index.astype(jnp.float32)
    shift_real = (1.0 - decay_ratio * jnp.cos(angles))[None, :, None, None] - eigenvalues[None, None, None, :] + diagonal[:, None, None, None]
    shift_imag = (decay_ratio * jnp.sin(angles))[None, :, None, None]
    magnitude = shift_real * shift_real + shift_imag * shift_imag
    scaled_real = (modal[0] * shift_real + modal[1] * shift_imag) / magnitude
    scaled_imag = (modal[1] * shift_real - modal[0] * shift_imag) / magnitude
    scaled = jnp.concatenate([scaled_real, scaled_imag], axis=0).astype(jnp.bfloat16).reshape(-1, columns)
    back = to_space(scaled, eigenbasis).astype(jnp.bfloat16).reshape((2,) + layout)
    return back[0], back[1]


def reference(concentration, forcing, eigenbasis, eigenvalues, settle_table, fraction_class, bed_mask):
    fractions, length, row_count, columns = concentration.shape
    classes = settle_table.shape[0]
    onehot = (fraction_class[:, None] == jnp.arange(classes, dtype=jnp.int32)[None, :]).astype(jnp.float32)
    settling = jnp.sum(onehot * settle_table[None, :], axis=1)
    diagonal = 2.0 * VERTICAL_DIFFUSION + settling
    decay_ratio = CIRCULANT_ALPHA ** (1.0 / length)
    slice_index = jnp.arange(length, dtype=jnp.int32)
    slice_times = slice_index.astype(jnp.float32)
    scale_up = decay_ratio ** slice_times
    scale_down = decay_ratio ** (-slice_times)
    cosine_table, sine_table = twiddles(slice_index, slice_index, length)
    bed_cells = bed_mask.astype(jnp.float32)

    def one_fraction(inputs):
        current, target, velocity, shift_diag = inputs
        padded = jnp.pad(current, ((0, 0), (1, 1), (0, 0)))
        upper_row = padded[:, :-2]
        lower_row = padded[:, 2:]
        vertical = VERTICAL_DIFFUSION * (lower_row - 2.0 * current + upper_row) + velocity * (upper_row - current) - DEPOSITION * bed_cells[None] * current
        coupled = (jnp.dot(current.astype(jnp.bfloat16).reshape(-1, columns), eigenbasis, preferred_element_type=jnp.float32) * eigenvalues[None, :]).astype(jnp.bfloat16)
        along_x = to_space(coupled, eigenbasis).reshape(current.shape)
        earlier = jnp.concatenate([jnp.zeros((1, row_count, columns), jnp.float32), current[:-1]], axis=0)
        residual = target - (current - along_x - vertical - earlier)
        scaled = (scale_up[:, None, None] * residual).astype(jnp.bfloat16)
        real_part = apply_table(cosine_table, scaled[None])
        imag_part = -apply_table(sine_table, scaled[None])
        back_real, back_imag = solve_shifted(real_part, imag_part, slice_index, length, decay_ratio, eigenbasis, eigenvalues, shift_diag[None])
        relaxed = (apply_table(cosine_table, back_real) - apply_table(sine_table, back_imag))[0] / length
        return current + scale_down[:, None, None] * relaxed

    return lax.map(one_fraction, (concentration, forcing, settling, diagonal))
```

```python
import functools

import jax
import jax.numpy as jnp
from jax import lax
from jax.experimental import pallas as pl
from jax.experimental.pallas import tpu as pltpu
from jax.sharding import PartitionSpec as P

ALPHA = 0.5
DIFF = 0.06
DEPO = 0.1
MESH = pl.DeviceIdType.MESH
CHIPS = 8
F32, BF16 = jnp.float32, jnp.bfloat16


def nt(a, b):
    return lax.dot_general(a, b, (((1,), (1,)), ((), ())), preferred_element_type=F32)


def nn(a, b):
    return jnp.dot(a, b, preferred_element_type=F32)


def kernel(
    F, R, X, SP,
    table_s, class_s, c_h, f_h, e_h, lam_h, bed_h, out_h,
    c_v, f_v, e_v, lam_v, bed_v, cb_v, q_v, cp_v, rb_v, edge_v, halo_v, dinv_v, dp_v, cl_v,
    a_v, ar_v, p0_v, p1_v, cs_v, cr_v, bs_v, bf_v, bb_v, zs_v, wz_v, acc_v,
    ld, e_sem, h_ss, h_rs, a_ss, a_rs, c_ss, c_rs, bo_ss, bf_ss, bf_rs, bb_ss, bb_rs, z_ss, z_rs, o_sem,
):
    TN = X // CHIPS
    H = F // 2
    t = lax.axis_index("tm")
    sp = lax.axis_index("space")
    z, h = t // 2, t % 2
    partner = (z * 2 + 1 - h, sp)
    nxt = (((z + 1) % CHIPS) * 2 + h, sp)
    prv = (((z + CHIPS - 1) % CHIPS) * 2 + h, sp)
    below = (t, (sp + 1) % SP)
    above = (t, (sp + SP - 1) % SP)

    def cols(j):
        return pl.ds(pl.multiple_of(j * TN, TN), TN)

    def load_e(j):
        return pltpu.make_async_copy(e_h.at[:, cols(j)], e_v.at[:, cols(j)], e_sem.at[j])

    ld_c = pltpu.make_async_copy(c_h, c_v, ld.at[0])
    ld_l = pltpu.make_async_copy(lam_h, lam_v, ld.at[1])
    ld_f = pltpu.make_async_copy(f_h, f_v, ld.at[2])
    ld_b = pltpu.make_async_copy(bed_h, bed_v, ld.at[3])
    ld_c.start()
    ld_l.start()
    for j in range(CHIPS):
        load_e(j).start()
    ld_f.start()
    ld_b.start()

    barrier = pltpu.get_barrier_semaphore()
    for dev in (partner, nxt, prv, below, above):
        pl.semaphore_signal(barrier, inc=1, device_id=dev, device_id_type=MESH)

    ld_l.wait()
    settling = [table_s[class_s[f]] for f in range(F)]
    for j in range(CHIPS):
        for f in range(F):
            dinv_v[f, j] = 1.0 / (1.0 + 2.0 * DIFF + settling[f] - lam_v[:, j * TN:(j + 1) * TN])

    for i in range(H):
        base = dinv_v[H * h + i]
        power = base
        dp_v[1, i] = power
        for m in range(2, 2 * CHIPS + 1):
            power = power * base
            dp_v[m, i] = power
        cl_v[i] = 1.0 / (1.0 - ALPHA * power)

    ld_c.wait()
    cb_v[...] = c_v[...].astype(BF16)
    for f in range(F):
        edge_v[0, f:f + 1, :] = c_v[(f + 1) * R - 1:(f + 1) * R, :]
        edge_v[1, f:f + 1, :] = c_v[f * R:f * R + 1, :]

    def first(j, carry):
        load_e(j).wait()
        q = nn(cb_v[...], e_v[:, cols(j)])
        q_v[j] = q
        cp_v[:, cols(j)] = (q * lam_v[:, cols(j)]).astype(BF16)
        return carry

    lax.fori_loop(0, CHIPS, first, 0)

    pl.semaphore_wait(barrier, 5)

    def halo(i, dev):
        return pltpu.make_async_remote_copy(
            edge_v.at[i], halo_v.at[i], h_ss.at[i], h_rs.at[i], device_id=dev, device_id_type=MESH
        )

    halo(0, below).start()
    halo(1, above).start()
    ld_f.wait()
    ld_b.wait()

    row = lax.broadcasted_iota(jnp.int32, (R, TN), 0)
    has_above = jnp.where(sp > 0, 1.0, 0.0).astype(F32)
    has_below = jnp.where(sp < SP - 1, 1.0, 0.0).astype(F32)

    halo(0, below).wait()
    halo(1, above).wait()

    def second(j, carry):
        along = nt(cp_v[...], e_v[cols(j), :])
        bed = DEPO * bed_v[:, cols(j)].astype(F32)
        for f in range(F):
            rows = slice(f * R, (f + 1) * R)
            c = c_v[rows, cols(j)]
            up = jnp.where(row == 0, halo_v[0, f:f + 1, cols(j)] * has_above, pltpu.roll(c, 1, 0))
            low = jnp.where(row == R - 1, halo_v[1, f:f + 1, cols(j)] * has_below, pltpu.roll(c, R - 1, 0))
            vert = DIFF * (low - 2.0 * c + up) + settling[f] * (up - c) - bed * c
            rest = f_v[rows, cols(j)] - (c - cb_v[rows, cols(j)].astype(F32)) + along[rows] + vert
            rb_v[rows, cols(j)] = rest.astype(BF16)
        return carry

    lax.fori_loop(0, CHIPS, second, 0)

    keep = jnp.where(t < 2 * CHIPS - 1, 1.0, 0.0).astype(F32)
    sigma = jnp.where(z == 0, ALPHA, 1.0).astype(F32)

    def chunk(s):
        return (z + CHIPS - s) % CHIPS

    def swap_a(k):
        return pltpu.make_async_remote_copy(
            a_v.at[k, pl.ds(H * (1 - h), H)], ar_v.at[k], a_ss.at[k], a_rs.at[k],
            device_id=partner, device_id_type=MESH,
        )

    def third(s):
        k = chunk(s)
        m = nn(rb_v[...], e_v[:, cols(k)])
        for f in range(F):
            rows = slice(f * R, (f + 1) * R)
            q = q_v[k, rows, :]
            a_v[k, f] = (m[rows] - q) * dinv_v[f, k] + keep * q
        swap_a(k).start()

    def chain(s, i):
        return pltpu.make_async_remote_copy(
            cs_v.at[s, i], cr_v.at[s, i], c_ss.at[s, i], c_rs.at[s, i],
            device_id=nxt, device_id_type=MESH,
        )

    def own_fwd(i):
        return pltpu.make_async_remote_copy(
            bs_v.at[i], bf_v.at[0, i], bo_ss.at[0, i], bf_rs.at[0, i],
            device_id=nxt, device_id_type=MESH,
        )

    def own_bwd(i):
        return pltpu.make_async_remote_copy(
            bs_v.at[i], bb_v.at[0, i], bo_ss.at[1, i], bb_rs.at[0, i],
            device_id=prv, device_id_type=MESH,
        )

    def relay_fwd(j, i):
        return pltpu.make_async_remote_copy(
            bf_v.at[j, i], bf_v.at[j + 1, i], bf_ss.at[j, i], bf_rs.at[j + 1, i],
            device_id=nxt, device_id_type=MESH,
        )

    def relay_bwd(j, i):
        return pltpu.make_async_remote_copy(
            bb_v.at[j, i], bb_v.at[j + 1, i], bb_ss.at[j, i], bb_rs.at[j + 1, i],
            device_id=prv, device_id_type=MESH,
        )

    def local(s, has_input):
        k = chunk(s)
        swap_a(k).wait_recv()
        for i in range(H):
            own, other = a_v[k, H * h + i], ar_v[k, i]
            a0 = jnp.where(h == 0, own, other)
            a1 = jnp.where(h == 0, other, own)
            d = dp_v[1, i, k]
            if has_input:
                chain(s - 1, i).wait_recv()
                a0 = a0 + (sigma * d) * cr_v[s - 1, i].astype(F32)
            p1 = a1 + d * a0
            p0_v[k, i] = a0
            p1_v[k, i] = p1
            yield i, p1

    third(0)
    third(1)
    for i, p1 in local(0, False):
        cs_v[0, i] = p1.astype(BF16)
        chain(0, i).start()

    def middle(s, carry):
        third(s + 1)
        for i, p1 in local(s, True):
            cs_v[s, i] = p1.astype(BF16)
            chain(s, i).start()
        return carry

    lax.fori_loop(1, CHIPS - 1, middle, 0)

    def swap_z(k, i):
        return pltpu.make_async_remote_copy(
            zs_v.at[k, i], wz_v.at[k, H * h + i], z_ss.at[k, i], z_rs.at[k, i],
            device_id=partner, device_id_type=MESH,
        )

    def stage(s, i, ze):
        k = chunk(s)
        wrap = jnp.where(s >= z, ALPHA, 1.0).astype(F32)
        ze = ze * wrap
        z0 = p0_v[k, i] + dp_v[2 * s + 1, i, k] * ze
        z1 = p1_v[k, i] + dp_v[2 * s + 2, i, k] * ze
        zs_v[k, i] = jnp.where(h == 0, z1, z0)
        swap_z(k, i).start()
        wz_v[k, H * h + i] = jnp.where(h == 0, z0, z1)

    def finish(s, base):
        k = chunk(s)
        for i in range(H):
            swap_z(k, i).wait_recv()
        w = jnp.concatenate(
            [wz_v[k, f] - keep * q_v[k, f * R:(f + 1) * R, :] for f in range(F)], axis=0
        ).astype(BF16)
        step = 2 * TN

        def part(n, carry):
            cs = pl.ds(pl.multiple_of(n * step, step), step)
            acc_v[:, cs] = base[:, cs] + nt(w, e_v[cs, cols(k)])
            return carry

        lax.fori_loop(0, X // step, part, 0)

    last = CHIPS - 1
    for i, p1 in local(last, True):
        ze = p1 * cl_v[i, chunk(last)]
        bs_v[i] = ze.astype(BF16)
        own_fwd(i).start()
        own_bwd(i).start()
        stage(last, i, ze)

    def got_fwd(j, relay):
        for i in range(H):
            (own_fwd(i) if j == 0 else relay_fwd(j - 1, i)).wait_recv()
            if relay:
                relay_fwd(j, i).start()
        for i in range(H):
            stage(j, i, bf_v[j, i].astype(F32))

    def got_bwd(j, relay):
        for i in range(H):
            (own_bwd(i) if j == 0 else relay_bwd(j - 1, i)).wait_recv()
            if relay:
                relay_bwd(j, i).start()
        for i in range(H):
            stage(CHIPS - 2 - j, i, bb_v[j, i].astype(F32))

    got_fwd(0, True)
    got_bwd(0, True)
    finish(last, c_v)
    got_fwd(1, True)
    got_bwd(1, True)
    finish(0, acc_v)
    finish(CHIPS - 2, acc_v)
    got_fwd(2, True)
    got_bwd(2, False)
    finish(1, acc_v)
    finish(CHIPS - 3, acc_v)
    got_fwd(3, False)
    finish(2, acc_v)
    finish(CHIPS - 4, acc_v)
    finish(3, acc_v)

    store = pltpu.make_async_copy(acc_v, out_h, o_sem)
    store.start()

    for k in range(CHIPS):
        swap_a(k).wait_send()
        for i in range(H):
            swap_z(k, i).wait_send()
    for i in range(H):
        for s in range(CHIPS - 1):
            chain(s, i).wait_send()
        own_fwd(i).wait_send()
        own_bwd(i).wait_send()
        for j in range(3):
            relay_fwd(j, i).wait_send()
        for j in range(2):
            relay_bwd(j, i).wait_send()
    store.wait()


def on_device(c, f, e, lam, table, cls, bed):
    F, S, R, X = c.shape
    SP = lax.axis_size("space")
    TN, H, M = X // CHIPS, F // 2, F * R
    any_spec = pl.BlockSpec(memory_space=pl.ANY)
    smem_spec = pl.BlockSpec(memory_space=pltpu.SMEM)
    dma = pltpu.SemaphoreType.DMA
    out = pl.pallas_call(
        functools.partial(kernel, F, R, X, SP),
        out_shape=jax.ShapeDtypeStruct((M, X), F32),
        in_specs=[smem_spec, smem_spec] + [any_spec] * 5,
        out_specs=any_spec,
        scratch_shapes=[
            pltpu.VMEM((M, X), F32),
            pltpu.VMEM((M, X), F32),
            pltpu.VMEM((X, X), BF16),
            pltpu.VMEM((1, X), F32),
            pltpu.VMEM((R, X), jnp.int32),
            pltpu.VMEM((M, X), BF16),
            pltpu.VMEM((CHIPS, M, TN), F32),
            pltpu.VMEM((M, X), BF16),
            pltpu.VMEM((M, X), BF16),
            pltpu.VMEM((2, F, X), F32),
            pltpu.VMEM((2, F, X), F32),
            pltpu.VMEM((F, CHIPS, 1, TN), F32),
            pltpu.VMEM((2 * CHIPS + 1, H, CHIPS, 1, TN), F32),
            pltpu.VMEM((H, CHIPS, 1, TN), F32),
            pltpu.VMEM((CHIPS, F, R, TN), F32),
            pltpu.VMEM((CHIPS, H, R, TN), F32),
            pltpu.VMEM((CHIPS, H, R, TN), F32),
            pltpu.VMEM((CHIPS, H, R, TN), F32),
            pltpu.VMEM((CHIPS - 1, H, R, TN), BF16),
            pltpu.VMEM((CHIPS - 1, H, R, TN), BF16),
            pltpu.VMEM((H, R, TN), BF16),
            pltpu.VMEM((4, H, R, TN), BF16),
            pltpu.VMEM((3, H, R, TN), BF16),
            pltpu.VMEM((CHIPS, H, R, TN), F32),
            pltpu.VMEM((CHIPS, F, R, TN), F32),
            pltpu.VMEM((M, X), F32),
            dma((4,)),
            dma((CHIPS,)),
            dma((2,)), dma((2,)),
            dma((CHIPS,)), dma((CHIPS,)),
            dma((CHIPS - 1, H)), dma((CHIPS - 1, H)),
            dma((2, H)),
            dma((3, H)), dma((4, H)),
            dma((2, H)), dma((3, H)),
            dma((CHIPS, H)), dma((CHIPS, H)),
            dma,
        ],
        compiler_params=pltpu.CompilerParams(
            collective_id=0, has_side_effects=True, vmem_limit_bytes=60 * 1024 * 1024
        ),
    )(
        table, cls, c.reshape(M, X), f.reshape(M, X), e, lam.reshape(1, X), bed,
    )
    return out.reshape(F, S, R, X)


def solution(mesh):
    return jax.shard_map(
        on_device,
        mesh=mesh,
        in_specs=(
            P(None, "tm", "space", None),
            P(None, "tm", "space", None),
            P(),
            P(),
            P(),
            P(),
            P("space", None),
        ),
        out_specs=P(None, "tm", "space", None),
        check_vma=False,
    )
```

```python
import functools

import jax
import jax.numpy as jnp
from jax import lax
from jax.experimental import pallas as pl
from jax.experimental.pallas import tpu as pltpu
from jax.sharding import PartitionSpec as P

ALPHA = 0.5
DIFF = 0.06
DEPO = 0.1
MESH = pl.DeviceIdType.MESH
ORDER = (4, 3, 5, 2, 6, 1, 7, 0)
CHIPS = 8
F32, BF16 = jnp.float32, jnp.bfloat16


def nt(a, b):
    return lax.dot_general(a, b, (((1,), (1,)), ((), ())), preferred_element_type=F32)


def nn(a, b):
    return jnp.dot(a, b, preferred_element_type=F32)


def kernel(
    F, R, X, SP,
    table_s, class_s, c_h, f_h, e_h, lam_h, bed_h, out_h,
    c_v, f_v, e_v, lam_v, bed_v, cb_v, q_v, cp_v, rb_v, edge_v, halo_v, dinv_v,
    a_v, ar_v, xs_v, xr_v, ys_v, yr_v, zs_v, wz_v, acc_v,
    ld, e_sem, h_ss, h_rs, a_ss, a_rs, g_ss, g_rs, s_ss, s_rs, z_ss, z_rs, o_sem,
):
    TN = X // CHIPS
    H = F // 2
    t = lax.axis_index("tm")
    sp = lax.axis_index("space")
    z, h = t // 2, t % 2
    partner = (z * 2 + 1 - h, sp)
    below = (t, (sp + 1) % SP)
    above = (t, (sp + SP - 1) % SP)

    def cols(j):
        return pl.ds(pl.multiple_of(j * TN, TN), TN)

    def load_e(j):
        return pltpu.make_async_copy(e_h.at[:, cols(j)], e_v.at[:, cols(j)], e_sem.at[j])

    ld_c = pltpu.make_async_copy(c_h, c_v, ld.at[0])
    ld_l = pltpu.make_async_copy(lam_h, lam_v, ld.at[1])
    ld_f = pltpu.make_async_copy(f_h, f_v, ld.at[2])
    ld_b = pltpu.make_async_copy(bed_h, bed_v, ld.at[3])
    ld_c.start()
    ld_l.start()
    for j in range(CHIPS):
        load_e(j).start()
    ld_f.start()
    ld_b.start()

    barrier = pltpu.get_barrier_semaphore()
    rest = [(((z + d) % CHIPS) * 2 + h, sp) for d in range(1, CHIPS)]
    for dev in [partner, below, above] + rest:
        pl.semaphore_signal(barrier, inc=1, device_id=dev, device_id_type=MESH)

    ld_l.wait()
    settling = [table_s[class_s[f]] for f in range(F)]
    for j in range(CHIPS):
        for f in range(F):
            dinv_v[f, j] = 1.0 / (1.0 + 2.0 * DIFF + settling[f] - lam_v[:, j * TN:(j + 1) * TN])

    ld_c.wait()
    cb_v[...] = c_v[...].astype(BF16)
    for f in range(F):
        edge_v[0, f:f + 1, :] = c_v[(f + 1) * R - 1:(f + 1) * R, :]
        edge_v[1, f:f + 1, :] = c_v[f * R:f * R + 1, :]

    def first(j, carry):
        load_e(j).wait()
        q = nn(cb_v[...], e_v[:, cols(j)])
        q_v[j] = q
        cp_v[:, cols(j)] = (q * lam_v[:, cols(j)]).astype(BF16)
        return carry

    lax.fori_loop(0, CHIPS, first, 0)

    pl.semaphore_wait(barrier, CHIPS + 2)

    def halo(i, dev):
        return pltpu.make_async_remote_copy(
            edge_v.at[i], halo_v.at[i], h_ss.at[i], h_rs.at[i], device_id=dev, device_id_type=MESH
        )

    halo(0, below).start()
    halo(1, above).start()
    ld_f.wait()
    ld_b.wait()

    row = lax.broadcasted_iota(jnp.int32, (R, TN), 0)
    has_above = jnp.where(sp > 0, 1.0, 0.0).astype(F32)
    has_below = jnp.where(sp < SP - 1, 1.0, 0.0).astype(F32)

    halo(0, below).wait()
    halo(1, above).wait()

    def second(j, carry):
        along = nt(cp_v[...], e_v[cols(j), :])
        bed = DEPO * bed_v[:, cols(j)].astype(F32)
        for f in range(F):
            rows = slice(f * R, (f + 1) * R)
            c = c_v[rows, cols(j)]
            up = jnp.where(row == 0, halo_v[0, f:f + 1, cols(j)] * has_above, pltpu.roll(c, 1, 0))
            low = jnp.where(row == R - 1, halo_v[1, f:f + 1, cols(j)] * has_below, pltpu.roll(c, R - 1, 0))
            vert = DIFF * (low - 2.0 * c + up) + settling[f] * (up - c) - bed * c
            rest = f_v[rows, cols(j)] - (c - cb_v[rows, cols(j)].astype(F32)) + along[rows] + vert
            rb_v[rows, cols(j)] = rest.astype(BF16)
        return carry

    lax.fori_loop(0, CHIPS, second, 0)

    keep = jnp.where(t < 2 * CHIPS - 1, 1.0, 0.0).astype(F32)
    sigma = jnp.where(z == 0, ALPHA, 1.0).astype(F32)

    def swap_a(k):
        return pltpu.make_async_remote_copy(
            a_v.at[k, pl.ds(H * (1 - h), H)], ar_v.at[k], a_ss.at[k], a_rs.at[k],
            device_id=partner, device_id_type=MESH,
        )

    def third(k):
        m = nn(rb_v[...], e_v[:, cols(k)])
        for f in range(F):
            rows = slice(f * R, (f + 1) * R)
            q = q_v[k, rows, :]
            a_v[k, f] = (m[rows] - q) * dinv_v[f, k] + keep * q
        swap_a(k).start()

    def chip(d):
        return (z + d) % CHIPS

    def gather(d, i):
        return pltpu.make_async_remote_copy(
            xs_v.at[d, i], xr_v.at[d, i], g_ss.at[d, i], g_rs.at[d, i],
            device_id=(chip(d) * 2 + h, sp), device_id_type=MESH,
        )

    def give(d, i):
        return pltpu.make_async_remote_copy(
            ys_v.at[d, i], yr_v.at[d, i], s_ss.at[d, i], s_rs.at[d, i],
            device_id=(chip(d) * 2 + h, sp), device_id_type=MESH,
        )

    def pair(k, i):
        own, other = a_v[k, H * h + i], ar_v[k, i]
        return jnp.where(h == 0, own, other), jnp.where(h == 0, other, own)

    def partial(d):
        k = chip(d)
        swap_a(k).wait_recv()
        for i in range(H):
            a0, a1 = pair(k, i)
            xs_v[d, i] = (a1 + dinv_v[H * h + i, k] * a0).astype(BF16)
            if d and i == 0:
                gather(d, 0).start()

    third(chip(ORDER[0]))
    for prev, d in zip(ORDER[:-1], ORDER[1:]):
        third(chip(d))
        partial(prev)
    partial(ORDER[-1])
    for i in range(1, H):
        for d in ORDER[:-1]:
            gather(d, i).start()

    def solve(i):
        d1 = dinv_v[H * h + i, z]
        d2 = d1 * d1
        d4 = d2 * d2
        d8 = d4 * d4
        for d in ORDER[:-1]:
            gather(d, i).wait_recv()
        xr_v[0, i] = xs_v[0, i]

        def part(c):
            return xr_v[(z - c + CHIPS) % CHIPS, i].astype(F32)

        total = part(0)
        for c in range(1, CHIPS):
            total = part(c) + d2 * total
        state = total / (1.0 - ALPHA * (d8 * d8))
        for c in range(CHIPS):
            ys_v[(c - z + CHIPS) % CHIPS, i] = state.astype(BF16)
            state = part(c) + d2 * (state * ALPHA if c == 0 else state)
        for d in ORDER[:-1]:
            give(d, i).start()
        yr_v[0, i] = ys_v[0, i]

    for i in range(H):
        solve(i)

    def swap_z(k, i):
        return pltpu.make_async_remote_copy(
            zs_v.at[k, i], wz_v.at[k, H * h + i], z_ss.at[k, i], z_rs.at[k, i],
            device_id=partner, device_id_type=MESH,
        )

    def stage(d):
        k = (z - d + CHIPS) % CHIPS
        for i in range(H):
            if d:
                give(d, i).wait_recv()
            a0, a1 = pair(k, i)
            d1 = dinv_v[H * h + i, k]
            z0 = a0 + (sigma * d1) * yr_v[d, i].astype(F32)
            z1 = a1 + d1 * z0
            zs_v[k, i] = jnp.where(h == 0, z1, z0)
            swap_z(k, i).start()
            wz_v[k, H * h + i] = jnp.where(h == 0, z0, z1)

    def finish(d, base):
        k = (z - d + CHIPS) % CHIPS
        for i in range(H):
            swap_z(k, i).wait_recv()
        w = jnp.concatenate(
            [wz_v[k, f] - keep * q_v[k, f * R:(f + 1) * R, :] for f in range(F)], axis=0
        ).astype(BF16)
        step = 2 * TN

        def part(n, carry):
            cs = pl.ds(pl.multiple_of(n * step, step), step)
            acc_v[:, cs] = base[:, cs] + nt(w, e_v[cs, cols(k)])
            return carry

        lax.fori_loop(0, X // step, part, 0)

    arrive = (0,) + ORDER[:-1]
    stage(arrive[0])
    for prev, d in zip(arrive[:-1], arrive[1:]):
        stage(d)
        finish(prev, c_v if prev == 0 else acc_v)
    finish(arrive[-1], acc_v)

    store = pltpu.make_async_copy(acc_v, out_h, o_sem)
    store.start()

    for k in range(CHIPS):
        swap_a(k).wait_send()
        for i in range(H):
            swap_z(k, i).wait_send()
    for d in ORDER[:-1]:
        for i in range(H):
            gather(d, i).wait_send()
            give(d, i).wait_send()
    store.wait()


def on_device(c, f, e, lam, table, cls, bed):
    F, S, R, X = c.shape
    SP = lax.axis_size("space")
    TN, H, M = X // CHIPS, F // 2, F * R
    any_spec = pl.BlockSpec(memory_space=pl.ANY)
    smem_spec = pl.BlockSpec(memory_space=pltpu.SMEM)
    dma = pltpu.SemaphoreType.DMA
    out = pl.pallas_call(
        functools.partial(kernel, F, R, X, SP),
        out_shape=jax.ShapeDtypeStruct((M, X), F32),
        in_specs=[smem_spec, smem_spec] + [any_spec] * 5,
        out_specs=any_spec,
        scratch_shapes=[
            pltpu.VMEM((M, X), F32),
            pltpu.VMEM((M, X), F32),
            pltpu.VMEM((X, X), BF16),
            pltpu.VMEM((1, X), F32),
            pltpu.VMEM((R, X), jnp.int32),
            pltpu.VMEM((M, X), BF16),
            pltpu.VMEM((CHIPS, M, TN), F32),
            pltpu.VMEM((M, X), BF16),
            pltpu.VMEM((M, X), BF16),
            pltpu.VMEM((2, F, X), F32),
            pltpu.VMEM((2, F, X), F32),
            pltpu.VMEM((F, CHIPS, 1, TN), F32),
            pltpu.VMEM((CHIPS, F, R, TN), F32),
            pltpu.VMEM((CHIPS, H, R, TN), F32),
            pltpu.VMEM((CHIPS, H, R, TN), BF16),
            pltpu.VMEM((CHIPS, H, R, TN), BF16),
            pltpu.VMEM((CHIPS, H, R, TN), BF16),
            pltpu.VMEM((CHIPS, H, R, TN), BF16),
            pltpu.VMEM((CHIPS, H, R, TN), F32),
            pltpu.VMEM((CHIPS, F, R, TN), F32),
            pltpu.VMEM((M, X), F32),
            dma((4,)),
            dma((CHIPS,)),
            dma((2,)), dma((2,)),
            dma((CHIPS,)), dma((CHIPS,)),
            dma((CHIPS, H)), dma((CHIPS, H)),
            dma((CHIPS, H)), dma((CHIPS, H)),
            dma((CHIPS, H)), dma((CHIPS, H)),
            dma,
        ],
        compiler_params=pltpu.CompilerParams(
            collective_id=0, has_side_effects=True, vmem_limit_bytes=60 * 1024 * 1024
        ),
    )(
        table, cls, c.reshape(M, X), f.reshape(M, X), e, lam.reshape(1, X), bed,
    )
    return out.reshape(F, S, R, X)


def solution(mesh):
    return jax.shard_map(
        on_device,
        mesh=mesh,
        in_specs=(
            P(None, "tm", "space", None),
            P(None, "tm", "space", None),
            P(),
            P(),
            P(),
            P(),
            P("space", None),
        ),
        out_specs=P(None, "tm", "space", None),
        check_vma=False,
    )
```

```python
import functools

import jax
import jax.numpy as jnp
from jax import lax
from jax.experimental import pallas as pl
from jax.experimental.pallas import tpu as pltpu
from jax.sharding import PartitionSpec as P

ALPHA = 0.5
DIFF = 0.06
DEPO = 0.1
MESH = pl.DeviceIdType.MESH
ORDER = (4, 3, 5, 2, 6, 1, 7, 0)
CHIPS = 8
EB = 16
EARLY = 2
AHEAD = 2
F32, BF16 = jnp.float32, jnp.bfloat16


def nt(a, b):
    return lax.dot_general(a, b, (((1,), (1,)), ((), ())), preferred_element_type=F32)


def nn(a, b):
    return jnp.dot(a, b, preferred_element_type=F32)


def kernel(
    F, R, X, SP,
    table_s, class_s, c_h, f_h, e_h, lam_h, bed_h, acc_v,
    c_v, f_v, e_v, lam_v, bed_v, cb_v, q_v, cp_v, rb_v, edge_v, halo_v, er_v, dinv_v,
    a_v, ar_v, xs_v, xr_v, ys_v, yr_v, zs_v, wz_v,
    ld, e_sem, h_ss, h_rs, a_ss, a_rs, g_ss, g_rs, s_ss, s_rs, z_ss, z_rs,
):
    TN = X // CHIPS
    H = F // 2
    t = lax.axis_index("tm")
    sp = lax.axis_index("space")
    z, h = t // 2, t % 2
    partner = (z * 2 + 1 - h, sp)
    below = (t, (sp + 1) % SP)
    above = (t, (sp + SP - 1) % SP)

    def cols(j):
        return pl.ds(pl.multiple_of(j * TN, TN), TN)

    def load_e(j):
        return pltpu.make_async_copy(e_h.at[:, cols(j)], e_v.at[:, cols(j)], e_sem.at[j])

    ld_c = pltpu.make_async_copy(c_h, c_v, ld.at[0])
    ld_l = pltpu.make_async_copy(lam_h, lam_v, ld.at[1])
    ld_f = pltpu.make_async_copy(f_h, f_v, ld.at[2])
    ld_b = pltpu.make_async_copy(bed_h, bed_v, ld.at[3])
    ld_c.start()
    ld_l.start()
    for j in range(CHIPS):
        load_e(j).start()
    ld_f.start()
    ld_b.start()

    barrier = pltpu.get_barrier_semaphore()
    rest = [(((z + d) % CHIPS) * 2 + h, sp) for d in range(1, CHIPS)]
    for dev in [partner, below, above] + rest:
        pl.semaphore_signal(barrier, inc=1, device_id=dev, device_id_type=MESH)

    ld_l.wait()
    settling = [table_s[class_s[f]] for f in range(F)]
    for j in range(CHIPS):
        for f in range(F):
            dinv_v[f, j] = 1.0 / (1.0 + 2.0 * DIFF + settling[f] - lam_v[:, j * TN:(j + 1) * TN])

    ld_c.wait()
    cb_v[...] = c_v[...].astype(BF16)
    for f in range(F):
        edge_v[0, f:f + 1, :] = c_v[(f + 1) * R - 1:(f + 1) * R, :]
        edge_v[1, f:f + 1, :] = c_v[f * R:f * R + 1, :]

    def first(j, carry):
        load_e(j).wait()
        q = nn(cb_v[...], e_v[:, cols(j)])
        q_v[j] = q
        cp_v[:, cols(j)] = (q * lam_v[:, cols(j)]).astype(BF16)
        return carry

    def halo(i, dev):
        return pltpu.make_async_remote_copy(
            edge_v.at[i], halo_v.at[i], h_ss.at[i], h_rs.at[i], device_id=dev, device_id_type=MESH
        )

    lax.fori_loop(0, EARLY, first, 0)
    pl.semaphore_wait(barrier, CHIPS + 2)
    halo(0, below).start()
    halo(1, above).start()
    lax.fori_loop(EARLY, CHIPS, first, 0)
    ld_f.wait()
    ld_b.wait()

    row = lax.broadcasted_iota(jnp.int32, (R, TN), 0)

    def second(j, carry):
        along = nt(cp_v[...], e_v[cols(j), :])
        bed = DEPO * bed_v[:, cols(j)].astype(F32)
        for f in range(F):
            rows = slice(f * R, (f + 1) * R)
            c = c_v[rows, cols(j)]
            up = jnp.where(row == 0, 0.0, pltpu.roll(c, 1, 0))
            low = jnp.where(row == R - 1, 0.0, pltpu.roll(c, R - 1, 0))
            vert = DIFF * (low - 2.0 * c + up) + settling[f] * (up - c) - bed * c
            rest = f_v[rows, cols(j)] - (c - cb_v[rows, cols(j)].astype(F32)) + along[rows] + vert
            rb_v[rows, cols(j)] = rest.astype(BF16)
            er_v[0, f, :, cols(j)] = rest[:EB]
            er_v[1, f, :, cols(j)] = rest[R - EB:]
        return carry

    lax.fori_loop(0, CHIPS, second, 0)

    halo(0, below).wait()
    halo(1, above).wait()
    has_above = jnp.where(sp > 0, 1.0, 0.0).astype(F32)
    has_below = jnp.where(sp < SP - 1, 1.0, 0.0).astype(F32)
    edge = lax.broadcasted_iota(jnp.int32, (EB, X), 0)
    for f in range(F):
        up = halo_v[0, f:f + 1, :] * ((DIFF + settling[f]) * has_above)
        rb_v[f * R:f * R + EB, :] = (er_v[0, f] + jnp.where(edge == 0, up, 0.0)).astype(BF16)
        low = halo_v[1, f:f + 1, :] * (DIFF * has_below)
        rb_v[(f + 1) * R - EB:(f + 1) * R, :] = (
            er_v[1, f] + jnp.where(edge == EB - 1, low, 0.0)
        ).astype(BF16)

    keep = jnp.where(t < 2 * CHIPS - 1, 1.0, 0.0).astype(F32)
    sigma = jnp.where(z == 0, ALPHA, 1.0).astype(F32)

    def swap_a(k):
        return pltpu.make_async_remote_copy(
            a_v.at[k, pl.ds(H * (1 - h), H)], ar_v.at[k], a_ss.at[k], a_rs.at[k],
            device_id=partner, device_id_type=MESH,
        )

    def third(k):
        m = nn(rb_v[...], e_v[:, cols(k)])
        for f in range(F):
            rows = slice(f * R, (f + 1) * R)
            q = q_v[k, rows, :]
            a_v[k, f] = (m[rows] - q) * dinv_v[f, k] + keep * q
        swap_a(k).start()

    def chip(d):
        return (z + d) % CHIPS

    def gather(d, i):
        return pltpu.make_async_remote_copy(
            xs_v.at[d, i], xr_v.at[d, i], g_ss.at[d, i], g_rs.at[d, i],
            device_id=(chip(d) * 2 + h, sp), device_id_type=MESH,
        )

    def give(d, i):
        return pltpu.make_async_remote_copy(
            ys_v.at[d, i], yr_v.at[d, i], s_ss.at[d, i], s_rs.at[d, i],
            device_id=(chip(d) * 2 + h, sp), device_id_type=MESH,
        )

    def pair(k, i):
        own, other = a_v[k, H * h + i], ar_v[k, i]
        return jnp.where(h == 0, own, other), jnp.where(h == 0, other, own)

    def partial(d):
        k = chip(d)
        swap_a(k).wait_recv()
        for i in range(H):
            a0, a1 = pair(k, i)
            xs_v[d, i] = (a1 + dinv_v[H * h + i, k] * a0).astype(BF16)
            if d and i == 0:
                gather(d, 0).start()

    for n in range(CHIPS + AHEAD):
        if n < CHIPS:
            third(chip(ORDER[n]))
        if n >= AHEAD:
            partial(ORDER[n - AHEAD])
    for i in range(1, H):
        for d in ORDER[:-1]:
            gather(d, i).start()

    def solve(i):
        d1 = dinv_v[H * h + i, z]
        d2 = d1 * d1
        d4 = d2 * d2
        d8 = d4 * d4
        for d in ORDER[:-1]:
            gather(d, i).wait_recv()
        xr_v[0, i] = xs_v[0, i]

        def part(c):
            return xr_v[(z - c + CHIPS) % CHIPS, i].astype(F32)

        total = part(0)
        for c in range(1, CHIPS):
            total = part(c) + d2 * total
        state = total / (1.0 - ALPHA * (d8 * d8))
        for c in range(CHIPS):
            ys_v[(c - z + CHIPS) % CHIPS, i] = state.astype(BF16)
            state = part(c) + d2 * (state * ALPHA if c == 0 else state)
        for d in ORDER[:-1]:
            give(d, i).start()
        yr_v[0, i] = ys_v[0, i]

    for i in range(H):
        solve(i)

    def swap_z(k, i):
        return pltpu.make_async_remote_copy(
            zs_v.at[k, i], wz_v.at[k, H * h + i], z_ss.at[k, i], z_rs.at[k, i],
            device_id=partner, device_id_type=MESH,
        )

    def stage(d):
        k = (z - d + CHIPS) % CHIPS
        for i in range(H):
            if d:
                give(d, i).wait_recv()
            a0, a1 = pair(k, i)
            d1 = dinv_v[H * h + i, k]
            z0 = a0 + (sigma * d1) * yr_v[d, i].astype(F32)
            z1 = a1 + d1 * z0
            zs_v[k, i] = jnp.where(h == 0, z1, z0)
            swap_z(k, i).start()
            wz_v[k, H * h + i] = jnp.where(h == 0, z0, z1)

    def finish(d, base):
        k = (z - d + CHIPS) % CHIPS
        for i in range(H):
            swap_z(k, i).wait_recv()
        w = jnp.concatenate(
            [wz_v[k, f] - keep * q_v[k, f * R:(f + 1) * R, :] for f in range(F)], axis=0
        ).astype(BF16)
        step = 2 * TN

        def part(n, carry):
            cs = pl.ds(pl.multiple_of(n * step, step), step)
            acc_v[:, cs] = base[:, cs] + nt(w, e_v[cs, cols(k)])
            return carry

        lax.fori_loop(0, X // step, part, 0)

    arrive = (0,) + ORDER[:-1]
    stage(arrive[0])
    for prev, d in zip(arrive[:-1], arrive[1:]):
        stage(d)
        finish(prev, c_v if prev == 0 else acc_v)
    finish(arrive[-1], acc_v)

    for k in range(CHIPS):
        swap_a(k).wait_send()
        for i in range(H):
            swap_z(k, i).wait_send()
    for d in ORDER[:-1]:
        for i in range(H):
            gather(d, i).wait_send()
            give(d, i).wait_send()


def on_device(c, f, e, lam, table, cls, bed):
    F, S, R, X = c.shape
    SP = lax.axis_size("space")
    TN, H, M = X // CHIPS, F // 2, F * R
    any_spec = pl.BlockSpec(memory_space=pltpu.HBM)
    smem_spec = pl.BlockSpec(memory_space=pltpu.SMEM)
    dma = pltpu.SemaphoreType.DMA
    out = pl.pallas_call(
        functools.partial(kernel, F, R, X, SP),
        out_shape=jax.ShapeDtypeStruct((M, X), F32),
        in_specs=[smem_spec, smem_spec] + [any_spec] * 5,
        out_specs=pl.BlockSpec(memory_space=pltpu.VMEM),
        scratch_shapes=[
            pltpu.VMEM((M, X), F32),
            pltpu.VMEM((M, X), F32),
            pltpu.VMEM((X, X), BF16),
            pltpu.VMEM((1, X), F32),
            pltpu.VMEM((R, X), jnp.int32),
            pltpu.VMEM((M, X), BF16),
            pltpu.VMEM((CHIPS, M, TN), F32),
            pltpu.VMEM((M, X), BF16),
            pltpu.VMEM((M, X), BF16),
            pltpu.VMEM((2, F, X), F32),
            pltpu.VMEM((2, F, X), F32),
            pltpu.VMEM((2, F, EB, X), F32),
            pltpu.VMEM((F, CHIPS, 1, TN), F32),
            pltpu.VMEM((CHIPS, F, R, TN), F32),
            pltpu.VMEM((CHIPS, H, R, TN), F32),
            pltpu.VMEM((CHIPS, H, R, TN), BF16),
            pltpu.VMEM((CHIPS, H, R, TN), BF16),
            pltpu.VMEM((CHIPS, H, R, TN), BF16),
            pltpu.VMEM((CHIPS, H, R, TN), BF16),
            pltpu.VMEM((CHIPS, H, R, TN), F32),
            pltpu.VMEM((CHIPS, F, R, TN), F32),
            dma((4,)),
            dma((CHIPS,)),
            dma((2,)), dma((2,)),
            dma((CHIPS,)), dma((CHIPS,)),
            dma((CHIPS, H)), dma((CHIPS, H)),
            dma((CHIPS, H)), dma((CHIPS, H)),
            dma((CHIPS, H)), dma((CHIPS, H)),
        ],
        compiler_params=pltpu.CompilerParams(
            collective_id=0, has_side_effects=True, vmem_limit_bytes=57 * 1024 * 1024
        ),
    )(
        table, cls, c.reshape(M, X), f.reshape(M, X), e, lam.reshape(1, X), bed,
    )
    return out.reshape(F, S, R, X)


def solution(mesh):
    return jax.shard_map(
        on_device,
        mesh=mesh,
        in_specs=(
            P(None, "tm", "space", None),
            P(None, "tm", "space", None),
            P(),
            P(),
            P(),
            P(),
            P("space", None),
        ),
        out_specs=P(None, "tm", "space", None),
        check_vma=False,
    )
```

```python
import functools

import jax
import jax.numpy as jnp
from jax import lax
from jax.experimental import pallas as pl
from jax.experimental.pallas import tpu as pltpu
from jax.sharding import PartitionSpec as P

ALPHA = 0.5
DIFF = 0.06
DEPO = 0.1
MESH = pl.DeviceIdType.MESH
ORDER = (4, 3, 5, 2, 6, 1, 7, 0)
CHIPS = 8
EARLY = 2
AHEAD = 2
F32, BF16 = jnp.float32, jnp.bfloat16


def PIECES(R):
    edge = R // 4
    return (0, edge, 2 * edge, 0), (1, 0, edge, 0), (1, R - edge, edge, edge)


def nt(a, b):
    return lax.dot_general(a, b, (((1,), (1,)), ((), ())), preferred_element_type=F32)


def nn(a, b):
    return jnp.dot(a, b, preferred_element_type=F32)


def kernel(
    F, R, X, SP,
    table_s, class_s, c_h, f_h, e_h, lam_h, bed_h, acc_v,
    c_v, f_v, e_v, lam_v, bed_v, cb_v, q_v, cp_v, rb_v, edge_v, halo_v, dinv_v,
    a_v, ar_v, xs_v, xr_v, ys_v, yr_v, zs_v, wz_v,
    ld, e_sem, h_ss, h_rs, a_ss, a_rs, g_ss, g_rs, s_ss, s_rs, z_ss, z_rs,
):
    TN = X // CHIPS
    H = F // 2
    RG, EB = R // 2, R // 4
    MG = F * RG
    t = lax.axis_index("tm")
    sp = lax.axis_index("space")
    z, h = t // 2, t % 2
    partner = (z * 2 + 1 - h, sp)
    below = (t, (sp + 1) % SP)
    above = (t, (sp + SP - 1) % SP)

    def cols(j):
        return pl.ds(pl.multiple_of(j * TN, TN), TN)

    def load_e(j):
        return pltpu.make_async_copy(e_h.at[:, cols(j)], e_v.at[:, cols(j)], e_sem.at[j])

    ld_c = pltpu.make_async_copy(c_h, c_v, ld.at[0])
    ld_l = pltpu.make_async_copy(lam_h, lam_v, ld.at[1])
    ld_f = pltpu.make_async_copy(f_h, f_v, ld.at[2])
    ld_b = pltpu.make_async_copy(bed_h, bed_v, ld.at[3])
    barrier = pltpu.get_barrier_semaphore()
    rest = [(((z + d) % CHIPS) * 2 + h, sp) for d in range(1, CHIPS)]
    for dev in [partner, below, above] + rest:
        pl.semaphore_signal(barrier, inc=1, device_id=dev, device_id_type=MESH)

    ld_c.start()
    ld_l.start()
    for j in range(CHIPS):
        load_e(j).start()
    ld_f.start()
    ld_b.start()

    ld_l.wait()
    settling = [table_s[class_s[f]] for f in range(F)]
    for j in range(CHIPS):
        for f in range(F):
            dinv_v[f, j] = 1.0 / (1.0 + 2.0 * DIFF + settling[f] - lam_v[:, j * TN:(j + 1) * TN])

    ld_c.wait()
    for f in range(F):
        for g, src, n, off in PIECES(R):
            dst = g * MG + f * RG + off
            cb_v[dst:dst + n, :] = c_v[f * R + src:f * R + src + n, :].astype(BF16)
        edge_v[0, f:f + 1, :] = c_v[(f + 1) * R - 1:(f + 1) * R, :]
        edge_v[1, f:f + 1, :] = c_v[f * R:f * R + 1, :]

    def first(j, carry):
        load_e(j).wait()
        q = nn(cb_v[...], e_v[:, cols(j)])
        q_v[j] = q
        cp_v[:, cols(j)] = (q * lam_v[:, cols(j)]).astype(BF16)
        return carry

    def halo(i, dev):
        return pltpu.make_async_remote_copy(
            edge_v.at[i], halo_v.at[i], h_ss.at[i], h_rs.at[i], device_id=dev, device_id_type=MESH
        )

    lax.fori_loop(0, EARLY, first, 0)
    pl.semaphore_wait(barrier, CHIPS + 2)
    halo(0, below).start()
    halo(1, above).start()
    lax.fori_loop(EARLY, CHIPS, first, 0)
    ld_f.wait()
    ld_b.wait()

    has_above = jnp.where(sp > 0, 1.0, 0.0).astype(F32)
    has_below = jnp.where(sp < SP - 1, 1.0, 0.0).astype(F32)

    def second(g):
        def tile(j, carry):
            along = nt(cp_v[g * MG:(g + 1) * MG, :], e_v[cols(j), :])
            for f in range(F):
                for piece, src, n, off in PIECES(R):
                    if piece != g:
                        continue
                    lo, hi = max(src - 8, 0), min(src + n + 8, R)
                    wide = c_v[f * R + lo:f * R + hi, cols(j)]
                    inner = slice(src - lo, src - lo + n)
                    c = wide[inner]
                    up = pltpu.roll(wide, 1, 0)[inner]
                    low = pltpu.roll(wide, hi - lo - 1, 0)[inner]
                    row = lax.broadcasted_iota(jnp.int32, (n, TN), 0)
                    if src == 0:
                        up = jnp.where(row == 0, halo_v[0, f:f + 1, cols(j)] * has_above, up)
                    if src + n == R:
                        low = jnp.where(row == n - 1, halo_v[1, f:f + 1, cols(j)] * has_below, low)
                    bed = DEPO * bed_v[src:src + n, cols(j)].astype(F32)
                    vert = DIFF * (low - 2.0 * c + up) + settling[f] * (up - c) - bed * c
                    dst = g * MG + f * RG + off
                    kept = c - cb_v[dst:dst + n, cols(j)].astype(F32)
                    rest = f_v[f * R + src:f * R + src + n, cols(j)] - kept + vert
                    rest = rest + along[f * RG + off:f * RG + off + n]
                    rb_v[dst:dst + n, cols(j)] = rest.astype(BF16)
            return carry

        lax.fori_loop(0, CHIPS, tile, 0)

    keep = jnp.where(t < 2 * CHIPS - 1, 1.0, 0.0).astype(F32)
    sigma = jnp.where(z == 0, ALPHA, 1.0).astype(F32)

    def swap_a(g, k):
        return pltpu.make_async_remote_copy(
            a_v.at[k, g, pl.ds(H * (1 - h), H)], ar_v.at[k, g], a_ss.at[k, g], a_rs.at[k, g],
            device_id=partner, device_id_type=MESH,
        )

    def third(g, k):
        m = nn(rb_v[g * MG:(g + 1) * MG, :], e_v[:, cols(k)])
        for f in range(F):
            q = q_v[k, g * MG + f * RG:g * MG + (f + 1) * RG, :]
            a_v[k, g, f] = (m[f * RG:(f + 1) * RG] - q) * dinv_v[f, k] + keep * q
        swap_a(g, k).start()

    def chip(d):
        return (z + d) % CHIPS

    def gather(d, g):
        return pltpu.make_async_remote_copy(
            xs_v.at[d, g], xr_v.at[d, g], g_ss.at[d, g], g_rs.at[d, g],
            device_id=(chip(d) * 2 + h, sp), device_id_type=MESH,
        )

    def give(d, g):
        return pltpu.make_async_remote_copy(
            ys_v.at[d, g], yr_v.at[d, g], s_ss.at[d, g], s_rs.at[d, g],
            device_id=(chip(d) * 2 + h, sp), device_id_type=MESH,
        )

    def pair(g, k, i):
        own, other = a_v[k, g, H * h + i], ar_v[k, g, i]
        return jnp.where(h == 0, own, other), jnp.where(h == 0, other, own)

    def partial(g, d):
        k = chip(d)
        swap_a(g, k).wait_recv()
        for i in range(H):
            a0, a1 = pair(g, k, i)
            xs_v[d, g, i] = (a1 + dinv_v[H * h + i, k] * a0).astype(BF16)
        if d:
            gather(d, g).start()

    def send(g):
        second(g)
        for n in range(CHIPS + AHEAD):
            if n < CHIPS:
                third(g, chip(ORDER[n]))
            if n >= AHEAD:
                partial(g, ORDER[n - AHEAD])

    send(0)
    halo(0, below).wait()
    halo(1, above).wait()
    send(1)

    def solve(g):
        for d in ORDER[:-1]:
            gather(d, g).wait_recv()
        xr_v[0, g] = xs_v[0, g]
        for i in range(H):
            d1 = dinv_v[H * h + i, z]
            d2 = d1 * d1
            d4 = d2 * d2
            d8 = d4 * d4

            def part(c):
                return xr_v[(z - c + CHIPS) % CHIPS, g, i].astype(F32)

            total = part(0)
            for c in range(1, CHIPS):
                total = part(c) + d2 * total
            state = total / (1.0 - ALPHA * (d8 * d8))
            for c in range(CHIPS):
                ys_v[(c - z + CHIPS) % CHIPS, g, i] = state.astype(BF16)
                state = part(c) + d2 * (state * ALPHA if c == 0 else state)
        for d in ORDER[:-1]:
            give(d, g).start()
        yr_v[0, g] = ys_v[0, g]

    solve(0)
    solve(1)

    def swap_z(g, k):
        return pltpu.make_async_remote_copy(
            zs_v.at[k, g], wz_v.at[k, g, pl.ds(H * h, H)], z_ss.at[k, g], z_rs.at[k, g],
            device_id=partner, device_id_type=MESH,
        )

    def stage(g, d):
        k = (z - d + CHIPS) % CHIPS
        if d:
            give(d, g).wait_recv()
        for i in range(H):
            a0, a1 = pair(g, k, i)
            d1 = dinv_v[H * h + i, k]
            z0 = a0 + (sigma * d1) * yr_v[d, g, i].astype(F32)
            z1 = a1 + d1 * z0
            zs_v[k, g, i] = jnp.where(h == 0, z1, z0)
            wz_v[k, g, H * h + i] = jnp.where(h == 0, z0, z1)
        swap_z(g, k).start()

    def finish(d, base):
        k = (z - d + CHIPS) % CHIPS
        for g in range(2):
            swap_z(g, k).wait_recv()
        blocks = []
        for f in range(F):
            w = [
                wz_v[k, g, f] - keep * q_v[k, g * MG + f * RG:g * MG + (f + 1) * RG, :]
                for g in range(2)
            ]
            blocks += [w[1][:EB], w[0], w[1][EB:]]
        w = jnp.concatenate(blocks, axis=0).astype(BF16)
        step = 2 * TN

        def part(n, carry):
            cs = pl.ds(pl.multiple_of(n * step, step), step)
            acc_v[:, cs] = base[:, cs] + nt(w, e_v[cs, cols(k)])
            return carry

        lax.fori_loop(0, X // step, part, 0)

    arrive = (0,) + ORDER[:-1]
    for d in arrive:
        stage(0, d)
    stage(1, arrive[0])
    for prev, d in zip(arrive[:-1], arrive[1:]):
        stage(1, d)
        finish(prev, c_v if prev == 0 else acc_v)
    finish(arrive[-1], acc_v)

    for g in range(2):
        for k in range(CHIPS):
            swap_a(g, k).wait_send()
            swap_z(g, k).wait_send()
        for d in ORDER[:-1]:
            gather(d, g).wait_send()
            give(d, g).wait_send()


def on_device(c, f, e, lam, table, cls, bed):
    F, S, R, X = c.shape
    SP = lax.axis_size("space")
    TN, H, M = X // CHIPS, F // 2, F * R
    any_spec = pl.BlockSpec(memory_space=pltpu.HBM)
    smem_spec = pl.BlockSpec(memory_space=pltpu.SMEM)
    dma = pltpu.SemaphoreType.DMA
    out = pl.pallas_call(
        functools.partial(kernel, F, R, X, SP),
        out_shape=jax.ShapeDtypeStruct((M, X), F32),
        in_specs=[smem_spec, smem_spec] + [any_spec] * 5,
        out_specs=pl.BlockSpec(memory_space=pltpu.VMEM),
        scratch_shapes=[
            pltpu.VMEM((M, X), F32),
            pltpu.VMEM((M, X), F32),
            pltpu.VMEM((X, X), BF16),
            pltpu.VMEM((1, X), F32),
            pltpu.VMEM((R, X), jnp.int32),
            pltpu.VMEM((M, X), BF16),
            pltpu.VMEM((CHIPS, M, TN), F32),
            pltpu.VMEM((M, X), BF16),
            pltpu.VMEM((M, X), BF16),
            pltpu.VMEM((2, F, X), F32),
            pltpu.VMEM((2, F, X), F32),
            pltpu.VMEM((F, CHIPS, 1, TN), F32),
            pltpu.VMEM((CHIPS, 2, F, R // 2, TN), F32),
            pltpu.VMEM((CHIPS, 2, H, R // 2, TN), F32),
            pltpu.VMEM((CHIPS, 2, H, R // 2, TN), BF16),
            pltpu.VMEM((CHIPS, 2, H, R // 2, TN), BF16),
            pltpu.VMEM((CHIPS, 2, H, R // 2, TN), BF16),
            pltpu.VMEM((CHIPS, 2, H, R // 2, TN), BF16),
            pltpu.VMEM((CHIPS, 2, H, R // 2, TN), F32),
            pltpu.VMEM((CHIPS, 2, F, R // 2, TN), F32),
            dma((4,)),
            dma((CHIPS,)),
            dma((2,)), dma((2,)),
            dma((CHIPS, 2)), dma((CHIPS, 2)),
            dma((CHIPS, 2)), dma((CHIPS, 2)),
            dma((CHIPS, 2)), dma((CHIPS, 2)),
            dma((CHIPS, 2)), dma((CHIPS, 2)),
        ],
        compiler_params=pltpu.CompilerParams(
            collective_id=0, has_side_effects=True, vmem_limit_bytes=57 * 1024 * 1024
        ),
    )(
        table, cls, c.reshape(M, X), f.reshape(M, X), e, lam.reshape(1, X), bed,
    )
    return out.reshape(F, S, R, X)


def solution(mesh):
    return jax.shard_map(
        on_device,
        mesh=mesh,
        in_specs=(
            P(None, "tm", "space", None),
            P(None, "tm", "space", None),
            P(),
            P(),
            P(),
            P(),
            P("space", None),
        ),
        out_specs=P(None, "tm", "space", None),
        check_vma=False,
    )
```

```python
import functools

import jax
import jax.numpy as jnp
from jax import lax
from jax.experimental import pallas as pl
from jax.experimental.pallas import tpu as pltpu
from jax.sharding import PartitionSpec as P

ALPHA = 0.5
DIFF = 0.06
DEPO = 0.1
MESH = pl.DeviceIdType.MESH
ORDER = (4, 3, 5, 2, 6, 1, 7, 0)
NEAR = (1, 7, 2, 6, 3, 5, 4)
CHIPS = 8
EARLY = 2
AHEAD = 2
F32, BF16 = jnp.float32, jnp.bfloat16


def PIECES(R):
    edge = R // 4
    return (0, edge, 2 * edge, 0), (1, 0, edge, 0), (1, R - edge, edge, edge)


def nt(a, b):
    return lax.dot_general(a, b, (((1,), (1,)), ((), ())), preferred_element_type=F32)


def nn(a, b):
    return jnp.dot(a, b, preferred_element_type=F32)


def kernel(
    F, R, X, SP,
    table_s, class_s, c_h, f_h, e_h, lam_h, bed_h, acc_v,
    c_v, f_v, e_v, lam_v, bed_v, cb_v, q_v, cp_v, rb_v, edge_v, halo_v, hr_v, dinv_v,
    a_v, ar_v, xs_v, xr_v, ys_v, yr_v, zs_v, wz_v,
    ld, e_sem, h_ss, h_rs, a_ss, a_rs, g_ss, g_rs, s_ss, s_rs, z_ss, z_rs,
):
    TN = X // CHIPS
    H = F // 2
    RG, EB = R // 2, R // 4
    MG = F * RG
    t = lax.axis_index("tm")
    sp = lax.axis_index("space")
    z, h = t // 2, t % 2
    partner = (z * 2 + 1 - h, sp)
    below = (t, (sp + 1) % SP)
    above = (t, (sp + SP - 1) % SP)

    def cols(j):
        return pl.ds(pl.multiple_of(j * TN, TN), TN)

    def load_e(j):
        return pltpu.make_async_copy(e_h.at[:, cols(j)], e_v.at[:, cols(j)], e_sem.at[j])

    ld_c = pltpu.make_async_copy(c_h, c_v, ld.at[0])
    ld_l = pltpu.make_async_copy(lam_h, lam_v, ld.at[1])
    ld_f = pltpu.make_async_copy(f_h, f_v, ld.at[2])
    ld_b = pltpu.make_async_copy(bed_h, bed_v, ld.at[3])
    barrier = pltpu.get_barrier_semaphore()
    rest = [(((z + d) % CHIPS) * 2 + h, sp) for d in range(1, CHIPS)]
    for dev in [partner, below, above] + rest:
        pl.semaphore_signal(barrier, inc=1, device_id=dev, device_id_type=MESH)

    ld_c.start()
    ld_l.start()
    for j in range(CHIPS):
        load_e(j).start()
    ld_f.start()
    ld_b.start()

    ld_l.wait()
    settling = [table_s[class_s[f]] for f in range(F)]
    for j in range(CHIPS):
        for f in range(F):
            dinv_v[f, j] = 1.0 / (1.0 + 2.0 * DIFF + settling[f] - lam_v[:, j * TN:(j + 1) * TN])

    ld_c.wait()
    for f in range(F):
        for g, src, n, off in PIECES(R):
            dst = g * MG + f * RG + off
            cb_v[dst:dst + n, :] = c_v[f * R + src:f * R + src + n, :].astype(BF16)
        edge_v[0, f:f + 1, :] = c_v[(f + 1) * R - 1:(f + 1) * R, :]
        edge_v[1, f:f + 1, :] = c_v[f * R:f * R + 1, :]

    def first(j, carry):
        load_e(j).wait()
        q = nn(cb_v[...], e_v[:, cols(j)])
        q_v[j] = q
        cp_v[:, cols(j)] = (q * lam_v[:, cols(j)]).astype(BF16)
        return carry

    def halo(i, dev):
        return pltpu.make_async_remote_copy(
            edge_v.at[i], halo_v.at[i], h_ss.at[i], h_rs.at[i], device_id=dev, device_id_type=MESH
        )

    lax.fori_loop(0, EARLY, first, 0)
    pl.semaphore_wait(barrier, CHIPS + 2)
    halo(0, below).start()
    halo(1, above).start()
    lax.fori_loop(EARLY, CHIPS, first, 0)
    ld_f.wait()
    ld_b.wait()

    def second(j, carry):
        along = nt(cp_v[...], e_v[cols(j), :])
        for f in range(F):
            for g, src, n, off in PIECES(R):
                lo, hi = max(src - 8, 0), min(src + n + 8, R)
                wide = c_v[f * R + lo:f * R + hi, cols(j)]
                inner = slice(src - lo, src - lo + n)
                c = wide[inner]
                up = pltpu.roll(wide, 1, 0)[inner]
                low = pltpu.roll(wide, hi - lo - 1, 0)[inner]
                row = lax.broadcasted_iota(jnp.int32, (n, TN), 0)
                if src == 0:
                    up = jnp.where(row == 0, 0.0, up)
                if src + n == R:
                    low = jnp.where(row == n - 1, 0.0, low)
                bed = DEPO * bed_v[src:src + n, cols(j)].astype(F32)
                vert = DIFF * (low - 2.0 * c + up) + settling[f] * (up - c) - bed * c
                dst = g * MG + f * RG + off
                kept = c - cb_v[dst:dst + n, cols(j)].astype(F32)
                rest = f_v[f * R + src:f * R + src + n, cols(j)] - kept + vert
                rb_v[dst:dst + n, cols(j)] = (rest + along[dst:dst + n]).astype(BF16)
        return carry

    lax.fori_loop(0, CHIPS, second, 0)

    keep = jnp.where(t < 2 * CHIPS - 1, 1.0, 0.0).astype(F32)
    sigma = jnp.where(z == 0, ALPHA, 1.0).astype(F32)

    def swap_a(g, k):
        return pltpu.make_async_remote_copy(
            a_v.at[k, g, pl.ds(H * (1 - h), H)], ar_v.at[k, g], a_ss.at[k, g], a_rs.at[k, g],
            device_id=partner, device_id_type=MESH,
        )

    def third(k):
        m = nn(rb_v[...], e_v[:, cols(k)])
        for g in range(2):
            for f in range(F):
                rows = slice(g * MG + f * RG, g * MG + (f + 1) * RG)
                q = q_v[k, rows, :]
                a_v[k, g, f] = (m[rows] - q) * dinv_v[f, k] + keep * q
        swap_a(0, k).start()

    def add_halo(k):
        m = nn(hr_v[...], e_v[:, cols(k)])
        row = lax.broadcasted_iota(jnp.int32, (8, TN), 0)
        for f in range(F):
            up = m[f:f + 1] * dinv_v[f, k]
            low = m[F + f:F + f + 1] * dinv_v[f, k]
            a_v[k, 1, f, 0:8] = a_v[k, 1, f, 0:8] + jnp.where(row == 0, up, 0.0)
            a_v[k, 1, f, RG - 8:RG] = a_v[k, 1, f, RG - 8:RG] + jnp.where(row == 7, low, 0.0)
        swap_a(1, k).start()

    def chip(d):
        return (z + d) % CHIPS

    def gather(d, g):
        return pltpu.make_async_remote_copy(
            xs_v.at[d, g], xr_v.at[d, g], g_ss.at[d, g], g_rs.at[d, g],
            device_id=(chip(d) * 2 + h, sp), device_id_type=MESH,
        )

    def give(d, g):
        return pltpu.make_async_remote_copy(
            ys_v.at[d, g], yr_v.at[d, g], s_ss.at[d, g], s_rs.at[d, g],
            device_id=(chip(d) * 2 + h, sp), device_id_type=MESH,
        )

    def pair(g, k, i):
        own, other = a_v[k, g, H * h + i], ar_v[k, g, i]
        return jnp.where(h == 0, own, other), jnp.where(h == 0, other, own)

    def partial(g, d):
        k = chip(d)
        swap_a(g, k).wait_recv()
        for i in range(H):
            a0, a1 = pair(g, k, i)
            xs_v[d, g, i] = (a1 + dinv_v[H * h + i, k] * a0).astype(BF16)
        if d:
            gather(d, g).start()

    def send(g, make):
        for n in range(CHIPS + AHEAD):
            if n < CHIPS:
                make(chip(ORDER[n]))
            if n >= AHEAD:
                partial(g, ORDER[n - AHEAD])

    send(0, third)
    halo(0, below).wait()
    halo(1, above).wait()
    has_above = jnp.where(sp > 0, 1.0, 0.0).astype(F32)
    has_below = jnp.where(sp < SP - 1, 1.0, 0.0).astype(F32)
    row = lax.broadcasted_iota(jnp.int32, (16, X), 0)
    edges = jnp.zeros((16, X), F32)
    for f in range(F):
        up = halo_v[0, f:f + 1, :] * ((DIFF + settling[f]) * has_above)
        low = halo_v[1, f:f + 1, :] * (DIFF * has_below)
        edges = jnp.where(row == f, up, jnp.where(row == F + f, low, edges))
    hr_v[...] = edges.astype(BF16)
    send(1, add_halo)

    def solve(g):
        for d in ORDER[:-1]:
            gather(d, g).wait_recv()
        xr_v[0, g] = xs_v[0, g]
        for i in range(H):
            d1 = dinv_v[H * h + i, z]
            d2 = d1 * d1
            d4 = d2 * d2
            d8 = d4 * d4

            def part(c):
                return xr_v[(z - c + CHIPS) % CHIPS, g, i].astype(F32)

            total = part(0)
            for c in range(1, CHIPS):
                total = part(c) + d2 * total
            state = total / (1.0 - ALPHA * (d8 * d8))
            for c in range(CHIPS):
                ys_v[(c - z + CHIPS) % CHIPS, g, i] = state.astype(BF16)
                state = part(c) + d2 * (state * ALPHA if c == 0 else state)
        for d in NEAR:
            give(d, g).start()
        yr_v[0, g] = ys_v[0, g]

    solve(0)
    solve(1)

    def swap_z(g, k):
        return pltpu.make_async_remote_copy(
            zs_v.at[k, g], wz_v.at[k, g, pl.ds(H * h, H)], z_ss.at[k, g], z_rs.at[k, g],
            device_id=partner, device_id_type=MESH,
        )

    def stage(g, d):
        k = (z - d + CHIPS) % CHIPS
        if d:
            give(d, g).wait_recv()
        for i in range(H):
            a0, a1 = pair(g, k, i)
            d1 = dinv_v[H * h + i, k]
            z0 = a0 + (sigma * d1) * yr_v[d, g, i].astype(F32)
            z1 = a1 + d1 * z0
            zs_v[k, g, i] = jnp.where(h == 0, z1, z0)
            wz_v[k, g, H * h + i] = jnp.where(h == 0, z0, z1)
        swap_z(g, k).start()

    def finish(d, base):
        k = (z - d + CHIPS) % CHIPS
        for g in range(2):
            swap_z(g, k).wait_recv()
        blocks = []
        for f in range(F):
            w = [
                wz_v[k, g, f] - keep * q_v[k, g * MG + f * RG:g * MG + (f + 1) * RG, :]
                for g in range(2)
            ]
            blocks += [w[1][:EB], w[0], w[1][EB:]]
        w = jnp.concatenate(blocks, axis=0).astype(BF16)
        step = 2 * TN

        def part(n, carry):
            cs = pl.ds(pl.multiple_of(n * step, step), step)
            acc_v[:, cs] = base[:, cs] + nt(w, e_v[cs, cols(k)])
            return carry

        lax.fori_loop(0, X // step, part, 0)

    arrive = (0,) + NEAR
    for d in arrive:
        stage(0, d)
    stage(1, arrive[0])
    for prev, d in zip(arrive[:-1], arrive[1:]):
        stage(1, d)
        finish(prev, c_v if prev == 0 else acc_v)
    finish(arrive[-1], acc_v)

    for g in range(2):
        for k in range(CHIPS):
            swap_a(g, k).wait_send()
            swap_z(g, k).wait_send()
        for d in ORDER[:-1]:
            gather(d, g).wait_send()
            give(d, g).wait_send()


def on_device(c, f, e, lam, table, cls, bed):
    F, S, R, X = c.shape
    SP = lax.axis_size("space")
    TN, H, M = X // CHIPS, F // 2, F * R
    any_spec = pl.BlockSpec(memory_space=pltpu.HBM)
    smem_spec = pl.BlockSpec(memory_space=pltpu.SMEM)
    dma = pltpu.SemaphoreType.DMA
    out = pl.pallas_call(
        functools.partial(kernel, F, R, X, SP),
        out_shape=jax.ShapeDtypeStruct((M, X), F32),
        in_specs=[smem_spec, smem_spec] + [any_spec] * 5,
        out_specs=pl.BlockSpec(memory_space=pltpu.VMEM),
        scratch_shapes=[
            pltpu.VMEM((M, X), F32),
            pltpu.VMEM((M, X), F32),
            pltpu.VMEM((X, X), BF16),
            pltpu.VMEM((1, X), F32),
            pltpu.VMEM((R, X), jnp.int32),
            pltpu.VMEM((M, X), BF16),
            pltpu.VMEM((CHIPS, M, TN), F32),
            pltpu.VMEM((M, X), BF16),
            pltpu.VMEM((M, X), BF16),
            pltpu.VMEM((2, F, X), F32),
            pltpu.VMEM((2, F, X), F32),
            pltpu.VMEM((16, X), BF16),
            pltpu.VMEM((F, CHIPS, 1, TN), F32),
            pltpu.VMEM((CHIPS, 2, F, R // 2, TN), F32),
            pltpu.VMEM((CHIPS, 2, H, R // 2, TN), F32),
            pltpu.VMEM((CHIPS, 2, H, R // 2, TN), BF16),
            pltpu.VMEM((CHIPS, 2, H, R // 2, TN), BF16),
            pltpu.VMEM((CHIPS, 2, H, R // 2, TN), BF16),
            pltpu.VMEM((CHIPS, 2, H, R // 2, TN), BF16),
            pltpu.VMEM((CHIPS, 2, H, R // 2, TN), F32),
            pltpu.VMEM((CHIPS, 2, F, R // 2, TN), F32),
            dma((4,)),
            dma((CHIPS,)),
            dma((2,)), dma((2,)),
            dma((CHIPS, 2)), dma((CHIPS, 2)),
            dma((CHIPS, 2)), dma((CHIPS, 2)),
            dma((CHIPS, 2)), dma((CHIPS, 2)),
            dma((CHIPS, 2)), dma((CHIPS, 2)),
        ],
        compiler_params=pltpu.CompilerParams(
            collective_id=0, has_side_effects=True, vmem_limit_bytes=57 * 1024 * 1024
        ),
    )(
        table, cls, c.reshape(M, X), f.reshape(M, X), e, lam.reshape(1, X), bed,
    )
    return out.reshape(F, S, R, X)


def solution(mesh):
    return jax.shard_map(
        on_device,
        mesh=mesh,
        in_specs=(
            P(None, "tm", "space", None),
            P(None, "tm", "space", None),
            P(),
            P(),
            P(),
            P(),
            P("space", None),
        ),
        out_specs=P(None, "tm", "space", None),
        check_vma=False,
    )
```

```python
import functools

import jax
import jax.numpy as jnp
from jax import lax
from jax.experimental import pallas as pl
from jax.experimental.pallas import tpu as pltpu
from jax.sharding import PartitionSpec as P

ALPHA = 0.5
DIFF = 0.06
DEPO = 0.1
MESH = pl.DeviceIdType.MESH
ORDER = (4, 3, 5, 2, 6, 1, 7, 0)
NEAR = (1, 7, 2, 6, 3, 5, 4)
GROUPS = ((0, 1, 7, 2), (6, 3, 5, 4))
CHIPS = 8
EARLY = 2
AHEAD = 2
F32, BF16 = jnp.float32, jnp.bfloat16


def PIECES(R):
    edge = R // 4
    return (0, edge, 2 * edge, 0), (1, 0, edge, 0), (1, R - edge, edge, edge)


def nt(a, b):
    return lax.dot_general(a, b, (((1,), (1,)), ((), ())), preferred_element_type=F32)


def nn(a, b):
    return jnp.dot(a, b, preferred_element_type=F32)


def kernel(
    F, R, X, SP,
    table_s, class_s, c_h, f_h, e_h, lam_h, bed_h, out_h,
    c_v, f_v, e_v, lam_v, bed_v, cb_v, q_v, cp_v, rb_v, edge_v, halo_v, hr_v, dinv_v,
    a_v, ar_v, xs_v, xr_v, ys_v, yr_v, zs_v, wz_v, w_v, acc_v,
    ld, e_sem, h_ss, h_rs, a_ss, a_rs, g_ss, g_rs, s_ss, s_rs, z_ss, z_rs, o_sem,
):
    TN = X // CHIPS
    H = F // 2
    RG, EB = R // 2, R // 4
    MG = F * RG
    t = lax.axis_index("tm")
    sp = lax.axis_index("space")
    z, h = t // 2, t % 2
    partner = (z * 2 + 1 - h, sp)
    below = (t, (sp + 1) % SP)
    above = (t, (sp + SP - 1) % SP)

    def cols(j):
        return pl.ds(pl.multiple_of(j * TN, TN), TN)

    def load_e(j):
        return pltpu.make_async_copy(e_h.at[:, cols(j)], e_v.at[:, cols(j)], e_sem.at[j])

    ld_c = pltpu.make_async_copy(c_h, c_v, ld.at[0])
    ld_l = pltpu.make_async_copy(lam_h, lam_v, ld.at[1])
    ld_f = pltpu.make_async_copy(f_h, f_v, ld.at[2])
    ld_b = pltpu.make_async_copy(bed_h, bed_v, ld.at[3])
    barrier = pltpu.get_barrier_semaphore()
    rest = [(((z + d) % CHIPS) * 2 + h, sp) for d in range(1, CHIPS)]
    for dev in [partner, below, above] + rest:
        pl.semaphore_signal(barrier, inc=1, device_id=dev, device_id_type=MESH)

    ld_c.start()
    ld_l.start()
    for j in range(CHIPS):
        load_e(j).start()
    ld_f.start()
    ld_b.start()

    ld_l.wait()
    settling = [table_s[class_s[f]] for f in range(F)]
    for j in range(CHIPS):
        for f in range(F):
            dinv_v[f, j] = 1.0 / (1.0 + 2.0 * DIFF + settling[f] - lam_v[:, j * TN:(j + 1) * TN])

    ld_c.wait()
    for f in range(F):
        for g, src, n, off in PIECES(R):
            dst = g * MG + f * RG + off
            cb_v[dst:dst + n, :] = c_v[f * R + src:f * R + src + n, :].astype(BF16)
        edge_v[0, f:f + 1, :] = c_v[(f + 1) * R - 1:(f + 1) * R, :]
        edge_v[1, f:f + 1, :] = c_v[f * R:f * R + 1, :]

    def first(j, carry):
        load_e(j).wait()
        q = nn(cb_v[...], e_v[:, cols(j)])
        q_v[j] = q
        cp_v[:, cols(j)] = (q * lam_v[:, cols(j)]).astype(BF16)
        return carry

    def halo(i, dev):
        return pltpu.make_async_remote_copy(
            edge_v.at[i], halo_v.at[i], h_ss.at[i], h_rs.at[i], device_id=dev, device_id_type=MESH
        )

    lax.fori_loop(0, EARLY, first, 0)
    pl.semaphore_wait(barrier, CHIPS + 2)
    halo(0, below).start()
    halo(1, above).start()
    lax.fori_loop(EARLY, CHIPS, first, 0)
    ld_f.wait()
    ld_b.wait()

    def second(j, carry):
        along = nt(cp_v[...], e_v[cols(j), :])
        for f in range(F):
            for g, src, n, off in PIECES(R):
                lo, hi = max(src - 8, 0), min(src + n + 8, R)
                wide = c_v[f * R + lo:f * R + hi, cols(j)]
                inner = slice(src - lo, src - lo + n)
                c = wide[inner]
                up = pltpu.roll(wide, 1, 0)[inner]
                low = pltpu.roll(wide, hi - lo - 1, 0)[inner]
                row = lax.broadcasted_iota(jnp.int32, (n, TN), 0)
                if src == 0:
                    up = jnp.where(row == 0, 0.0, up)
                if src + n == R:
                    low = jnp.where(row == n - 1, 0.0, low)
                bed = DEPO * bed_v[src:src + n, cols(j)].astype(F32)
                vert = DIFF * (low - 2.0 * c + up) + settling[f] * (up - c) - bed * c
                dst = g * MG + f * RG + off
                kept = c - cb_v[dst:dst + n, cols(j)].astype(F32)
                rest = f_v[f * R + src:f * R + src + n, cols(j)] - kept + vert
                rb_v[dst:dst + n, cols(j)] = (rest + along[dst:dst + n]).astype(BF16)
        return carry

    lax.fori_loop(0, CHIPS, second, 0)

    keep = jnp.where(t < 2 * CHIPS - 1, 1.0, 0.0).astype(F32)
    sigma = jnp.where(z == 0, ALPHA, 1.0).astype(F32)

    def swap_a(g, k):
        return pltpu.make_async_remote_copy(
            a_v.at[k, g, pl.ds(H * (1 - h), H)], ar_v.at[k, g], a_ss.at[k, g], a_rs.at[k, g],
            device_id=partner, device_id_type=MESH,
        )

    def third(k):
        m = nn(rb_v[...], e_v[:, cols(k)])
        for g in range(2):
            for f in range(F):
                rows = slice(g * MG + f * RG, g * MG + (f + 1) * RG)
                q = q_v[k, rows, :]
                a_v[k, g, f] = (m[rows] - q) * dinv_v[f, k] + keep * q
        swap_a(0, k).start()

    def add_halo(k):
        m = nn(hr_v[...], e_v[:, cols(k)])
        row = lax.broadcasted_iota(jnp.int32, (8, TN), 0)
        for f in range(F):
            up = m[f:f + 1] * dinv_v[f, k]
            low = m[F + f:F + f + 1] * dinv_v[f, k]
            a_v[k, 1, f, 0:8] = a_v[k, 1, f, 0:8] + jnp.where(row == 0, up, 0.0)
            a_v[k, 1, f, RG - 8:RG] = a_v[k, 1, f, RG - 8:RG] + jnp.where(row == 7, low, 0.0)
        swap_a(1, k).start()

    def chip(d):
        return (z + d) % CHIPS

    def gather(d, g):
        return pltpu.make_async_remote_copy(
            xs_v.at[d, g], xr_v.at[d, g], g_ss.at[d, g], g_rs.at[d, g],
            device_id=(chip(d) * 2 + h, sp), device_id_type=MESH,
        )

    def give(d, g):
        return pltpu.make_async_remote_copy(
            ys_v.at[d, g], yr_v.at[d, g], s_ss.at[d, g], s_rs.at[d, g],
            device_id=(chip(d) * 2 + h, sp), device_id_type=MESH,
        )

    def pair(g, k, i):
        own, other = a_v[k, g, H * h + i], ar_v[k, g, i]
        return jnp.where(h == 0, own, other), jnp.where(h == 0, other, own)

    def partial(g, d):
        k = chip(d)
        swap_a(g, k).wait_recv()
        for i in range(H):
            a0, a1 = pair(g, k, i)
            xs_v[d, g, i] = (a1 + dinv_v[H * h + i, k] * a0).astype(BF16)
        if d:
            gather(d, g).start()

    def send(g, make):
        for n in range(CHIPS + AHEAD):
            if n < CHIPS:
                make(chip(ORDER[n]))
            if n >= AHEAD:
                partial(g, ORDER[n - AHEAD])

    send(0, third)
    halo(0, below).wait()
    halo(1, above).wait()
    has_above = jnp.where(sp > 0, 1.0, 0.0).astype(F32)
    has_below = jnp.where(sp < SP - 1, 1.0, 0.0).astype(F32)
    row = lax.broadcasted_iota(jnp.int32, (16, X), 0)
    edges = jnp.zeros((16, X), F32)
    for f in range(F):
        up = halo_v[0, f:f + 1, :] * ((DIFF + settling[f]) * has_above)
        low = halo_v[1, f:f + 1, :] * (DIFF * has_below)
        edges = jnp.where(row == f, up, jnp.where(row == F + f, low, edges))
    hr_v[...] = edges.astype(BF16)
    send(1, add_halo)

    def solve(g):
        for d in ORDER[:-1]:
            gather(d, g).wait_recv()
        xr_v[0, g] = xs_v[0, g]
        for i in range(H):
            d1 = dinv_v[H * h + i, z]
            d2 = d1 * d1
            d4 = d2 * d2
            d8 = d4 * d4

            def part(c):
                return xr_v[(z - c + CHIPS) % CHIPS, g, i].astype(F32)

            total = part(0)
            for c in range(1, CHIPS):
                total = part(c) + d2 * total
            state = total / (1.0 - ALPHA * (d8 * d8))
            for c in range(CHIPS):
                ys_v[(c - z + CHIPS) % CHIPS, g, i] = state.astype(BF16)
                state = part(c) + d2 * (state * ALPHA if c == 0 else state)
        for d in NEAR:
            give(d, g).start()
        yr_v[0, g] = ys_v[0, g]

    solve(0)
    solve(1)

    def swap_z(g, k):
        return pltpu.make_async_remote_copy(
            zs_v.at[k, g], wz_v.at[k, g, pl.ds(H * h, H)], z_ss.at[k, g], z_rs.at[k, g],
            device_id=partner, device_id_type=MESH,
        )

    def stage(g, d):
        k = (z - d + CHIPS) % CHIPS
        if d:
            give(d, g).wait_recv()
        for i in range(H):
            a0, a1 = pair(g, k, i)
            d1 = dinv_v[H * h + i, k]
            z0 = a0 + (sigma * d1) * yr_v[d, g, i].astype(F32)
            z1 = a1 + d1 * z0
            zs_v[k, g, i] = jnp.where(h == 0, z1, z0)
            wz_v[k, g, H * h + i] = jnp.where(h == 0, z0, z1)
        swap_z(g, k).start()

    def ready(d):
        k = (z - d + CHIPS) % CHIPS
        for g in range(2):
            swap_z(g, k).wait_recv()
        blocks = []
        for f in range(F):
            w = [
                wz_v[k, g, f] - keep * q_v[k, g * MG + f * RG:g * MG + (f + 1) * RG, :]
                for g in range(2)
            ]
            blocks += [w[1][:EB], w[0], w[1][EB:]]
        w_v[d] = jnp.concatenate(blocks, axis=0).astype(BF16)

    step = 2 * TN

    def store(n):
        cs = pl.ds(pl.multiple_of(n * step, step), step)
        return pltpu.make_async_copy(acc_v.at[:, cs], out_h.at[:, cs], o_sem.at[n])

    def product(ds, base, last):

        def part(n, carry):
            cs = pl.ds(pl.multiple_of(n * step, step), step)
            total = base[:, cs]
            for d in ds:
                total = total + nt(w_v[d], e_v[cs, cols((z - d + CHIPS) % CHIPS)])
            acc_v[:, cs] = total
            if last:
                store(n).start()
            return carry

        lax.fori_loop(0, X // step, part, 0)

    for d in (0,) + NEAR:
        stage(0, d)
    base = c_v
    for group in GROUPS:
        for d in group:
            stage(1, d)
        for d in group:
            ready(d)
        product(group, base, group is GROUPS[-1])
        base = acc_v

    for g in range(2):
        for k in range(CHIPS):
            swap_a(g, k).wait_send()
            swap_z(g, k).wait_send()
        for d in ORDER[:-1]:
            gather(d, g).wait_send()
            give(d, g).wait_send()
    for n in range(CHIPS // 2):
        store(n).wait()


def on_device(c, f, e, lam, table, cls, bed):
    F, S, R, X = c.shape
    SP = lax.axis_size("space")
    TN, H, M = X // CHIPS, F // 2, F * R
    any_spec = pl.BlockSpec(memory_space=pltpu.HBM)
    smem_spec = pl.BlockSpec(memory_space=pltpu.SMEM)
    dma = pltpu.SemaphoreType.DMA
    out = pl.pallas_call(
        functools.partial(kernel, F, R, X, SP),
        out_shape=jax.ShapeDtypeStruct((M, X), F32),
        in_specs=[smem_spec, smem_spec] + [any_spec] * 5,
        out_specs=any_spec,
        scratch_shapes=[
            pltpu.VMEM((M, X), F32),
            pltpu.VMEM((M, X), F32),
            pltpu.VMEM((X, X), BF16),
            pltpu.VMEM((1, X), F32),
            pltpu.VMEM((R, X), jnp.int32),
            pltpu.VMEM((M, X), BF16),
            pltpu.VMEM((CHIPS, M, TN), F32),
            pltpu.VMEM((M, X), BF16),
            pltpu.VMEM((M, X), BF16),
            pltpu.VMEM((2, F, X), F32),
            pltpu.VMEM((2, F, X), F32),
            pltpu.VMEM((16, X), BF16),
            pltpu.VMEM((F, CHIPS, 1, TN), F32),
            pltpu.VMEM((CHIPS, 2, F, R // 2, TN), F32),
            pltpu.VMEM((CHIPS, 2, H, R // 2, TN), F32),
            pltpu.VMEM((CHIPS, 2, H, R // 2, TN), BF16),
            pltpu.VMEM((CHIPS, 2, H, R // 2, TN), BF16),
            pltpu.VMEM((CHIPS, 2, H, R // 2, TN), BF16),
            pltpu.VMEM((CHIPS, 2, H, R // 2, TN), BF16),
            pltpu.VMEM((CHIPS, 2, H, R // 2, TN), F32),
            pltpu.VMEM((CHIPS, 2, F, R // 2, TN), F32),
            pltpu.VMEM((CHIPS, M, TN), BF16),
            pltpu.VMEM((M, X), F32),
            dma((4,)),
            dma((CHIPS,)),
            dma((2,)), dma((2,)),
            dma((CHIPS, 2)), dma((CHIPS, 2)),
            dma((CHIPS, 2)), dma((CHIPS, 2)),
            dma((CHIPS, 2)), dma((CHIPS, 2)),
            dma((CHIPS, 2)), dma((CHIPS, 2)),
            dma((CHIPS // 2,)),
        ],
        compiler_params=pltpu.CompilerParams(
            collective_id=0, has_side_effects=True, vmem_limit_bytes=57 * 1024 * 1024
        ),
    )(
        table, cls, c.reshape(M, X), f.reshape(M, X), e, lam.reshape(1, X), bed,
    )
    return out.reshape(F, S, R, X)


def solution(mesh):
    return jax.shard_map(
        on_device,
        mesh=mesh,
        in_specs=(
            P(None, "tm", "space", None),
            P(None, "tm", "space", None),
            P(),
            P(),
            P(),
            P(),
            P("space", None),
        ),
        out_specs=P(None, "tm", "space", None),
        check_vma=False,
    )
```
